512 devices in a mesh: space: 32 (over z_lo, x, core), species: 16 (over y, z_hi).
Axes of the slice: x: 4, y: 4, z: 16 (z_hi: 4, z_lo: 4; z = z_hi * 4 + z_lo), core: 2. Of those that a mesh axis runs over, the one named last changes fastest.
Arguments:
- biomass: bfloat16 [512, 64, 1024], P('species', 'space'), may hold values from 0.019897461 to 1
- resources: float32 [128, 64, 1024], P('species', 'space'), may hold values from 0.1 to 4
- capacity: float32 [512, 128], P('species'), may hold values from 0.002 to 0.05
- affinity: float32 [512, 128], P('species'), may hold values from 0.2 to 5
- secretion: bfloat16 [128, 512], P(None, 'species'), may hold values from 0 to 0.059814453
- energy_yield: float32 [128], replicated, may hold values from 0.5 to 2
- maintenance: float32 [512], P('species'), may hold values from 0.3 to 3
- motility: float32 [512], P('species'), may hold values from 0.04 to 0.6
- diffusivity: float32 [128], P('species'), may hold values from 0.02 to 0.6
- supply: float32 [128], P('species'), may hold values from 0.4 to 4
Outputs:
- growth: float32 [512, 64, 1024], P('species', 'space')
- new_biomass: float32 [512, 64, 1024], P('species', 'space')
- new_resources: float32 [128, 64, 1024], P('species', 'space')
The draws below stay inside these ranges and needn't reach their ends.
All inputs are finite; a program needn't handle non-finite values.
Results may differ from the reference program's by a relative error of at most 0.0003.
Values may be sent and summed in bfloat16 or wider, within the bound.
A program may use at most 64 MiB of HBM per device.

```python
import math
import jax
import jax.numpy as jnp
from jax import lax

STRAINS = 512
RESOURCES = 128
NY = 16
NZ = 64
NX = 64
PLANE = 1024


def levels(key, dims, cuts, smallest, top_value):
    level, own = 1.0, jax.random.fold_in(key, 6)
    for dim, parts in cuts:
        draws = jnp.exp(jax.random.uniform(jax.random.fold_in(own, dim), (parts,), jnp.float32, smallest / len(cuts), top_value / len(cuts)))
        level = level * jnp.repeat(draws, dims[dim] // parts).reshape([-1 if axis == dim else 1 for axis in range(len(dims))])
    return level


def setup_inputs(seed: int = 0) -> dict:
    key_list = jax.random.split(jax.random.key(seed), 11)
    biomass = jnp.clip(jnp.exp(math.log(1.0) - 3.9171631 * jax.random.uniform(key_list[0], (STRAINS, NX, PLANE), jnp.float32) ** levels(key_list[0], (STRAINS, NX, PLANE), ((0, 16), (1, 32)), -0.2, 0.2)), 0.019897461, 1.0).astype(jnp.bfloat16)
    resources = jnp.clip(jnp.exp(math.log(4.0) - 3.6888794 * jax.random.uniform(key_list[1], (RESOURCES, NX, PLANE), jnp.float32) ** levels(key_list[1], (RESOURCES, NX, PLANE), ((0, 16), (1, 32)), -0.2, 0.2)), 0.1, 4.0)
    capacity = jnp.clip(jnp.exp(math.log(0.05) - 3.218876 * jax.random.uniform(key_list[2], (STRAINS, RESOURCES), jnp.float32) ** levels(key_list[2], (STRAINS, RESOURCES), ((0, 16),), -0.2, 0.2)), 0.002, 0.05)
    affinity = jnp.clip(jnp.exp(math.log(5.0) - 3.218876 * jax.random.uniform(key_list[3], (STRAINS, RESOURCES), jnp.float32) ** levels(key_list[3], (STRAINS, RESOURCES), ((0, 16),), -0.2, 0.2)), 0.2, 5.0)
    secretion = jnp.clip(0.059814453 * jax.random.uniform(key_list[4], (RESOURCES, STRAINS), jnp.float32) ** levels(key_list[4], (RESOURCES, STRAINS), ((1, 16),), -0.2, 0.2), 0.0, 0.059814453).astype(jnp.bfloat16)
    energy_yield = jnp.clip(jnp.exp(jax.random.uniform(key_list[5], (RESOURCES,), jnp.float32, math.log(0.5), math.log(2.0))), 0.5, 2.0)
    maintenance = jnp.clip(jnp.exp(math.log(3.0) - 2.3025851 * jax.random.uniform(key_list[6], (STRAINS,), jnp.float32) ** levels(key_list[6], (STRAINS,), ((0, 16),), -0.2, 0.2)), 0.3, 3.0)
    motility = jnp.clip(jnp.exp(math.log(0.6) - 2.7080503 * jax.random.uniform(key_list[7], (STRAINS,), jnp.float32) ** levels(key_list[7], (STRAINS,), ((0, 16),), -0.2, 0.2)), 0.04, 0.6)
    diffusivity = jnp.clip(jnp.exp(math.log(0.6) - 3.4011974 * jax.random.uniform(key_list[8], (RESOURCES,), jnp.float32) ** levels(key_list[8], (RESOURCES,), ((0, 16),), -0.2, 0.2)), 0.02, 0.6)
    supply = jnp.clip(jnp.exp(math.log(4.0) - 2.3025851 * jax.random.uniform(key_list[9], (RESOURCES,), jnp.float32) ** levels(key_list[9], (RESOURCES,), ((0, 16),), -0.2, 0.2)), 0.4, 4.0)
    return dict(biomass=biomass, resources=resources, capacity=capacity, affinity=affinity, secretion=secretion, energy_yield=energy_yield, maintenance=maintenance, motility=motility, diffusivity=diffusivity, supply=supply)


time_step = 0.25


def laplace(padded, depth_cells, width_cells):
    channel_count = padded.shape[0]
    inner_cells = padded[:, 1:-1, :]
    slab_rows = inner_cells.shape[1]
    block_view = inner_cells.reshape(channel_count, slab_rows, depth_cells, width_cells)
    extended = jnp.pad(block_view, ((0, 0), (0, 0), (1, 1), (1, 1)), mode="edge")
    beside_x = padded[:, 2:, :] + padded[:, :-2, :]
    beside_yz = extended[:, :, 2:, 1:-1] + extended[:, :, :-2, 1:-1] + extended[:, :, 1:-1, 2:] + extended[:, :, 1:-1, :-2]
    return beside_x + beside_yz.reshape(channel_count, slab_rows, -1) - 6.0 * inner_cells


def periodic(field):
    return jnp.concatenate([field[:, -1:, :], field, field[:, :1, :]], axis=1)


def reference(biomass, resources, capacity, affinity, secretion, energy_yield, maintenance, motility, diffusivity, supply):
    seen = lax.optimization_barrier(resources.astype(jnp.bfloat16)).astype(jnp.float32)
    seen_flat = seen.reshape(RESOURCES, -1)
    mass = biomass.astype(jnp.float32)
    mass_flat = mass.reshape(STRAINS, -1)
    cell_count = seen_flat.shape[1]

    def per_strain(carry, item):
        consumed, secreted = carry
        cap_row, aff_row, sec_col, mass_row, maint_value = item
        uptake = cap_row[:, None] * seen_flat / (aff_row[:, None] + seen_flat)
        growth_row = jnp.sum(energy_yield[:, None] * uptake, axis=0) - maint_value
        flux_row = jnp.sum(uptake, axis=0)
        rounded = lax.optimization_barrier((mass_row * flux_row).astype(jnp.bfloat16)).astype(jnp.float32)
        consumed = consumed + mass_row[None, :] * uptake
        secreted = secreted + sec_col.astype(jnp.float32)[:, None] * rounded[None, :]
        return (consumed, secreted), growth_row

    start_sums = (jnp.zeros((RESOURCES, cell_count), jnp.float32), jnp.zeros((RESOURCES, cell_count), jnp.float32))
    (consumed, secreted), growth_rows = lax.scan(per_strain, start_sums, (capacity, affinity, secretion.T, mass_flat, maintenance))
    growth = growth_rows.reshape(biomass.shape)
    spread_mass = motility[:, None, None] * laplace(periodic(mass), NY, NZ)
    new_biomass = mass + time_step * (mass * growth + spread_mass)
    spread_resources = diffusivity[:, None, None] * laplace(periodic(resources), NY, NZ)
    net_release = (secreted - consumed).reshape(resources.shape)
    new_resources = resources + time_step * (spread_resources + net_release + supply[:, None, None])
    return growth, new_biomass, new_resources
```

```python
import functools

import jax
import jax.numpy as jnp
from jax import lax
from jax.experimental import pallas as pl
from jax.experimental.pallas import tpu as pltpu
from jax.sharding import PartitionSpec as P

MESH = pl.DeviceIdType.MESH
RING = 4
PARTS = 4
TIME_STEP = 0.25
ROWS = 16
LANES = 128


def laplace(field, low, high):
    row = lax.broadcasted_iota(jnp.int32, (ROWS, LANES), 0)
    lane = lax.broadcasted_iota(jnp.int32, (ROWS, LANES), 1)
    odd = lax.rem(row, 2) == 1
    z = lax.rem(lane, 64)
    both = field + jnp.where(odd, low, high)
    beside_x = jnp.where(odd, pltpu.roll(both, 1, 0), pltpu.roll(both, ROWS - 1, 0))
    up = jnp.where(z == 63, field, pltpu.roll(field, LANES - 1, 1))
    down = jnp.where(z == 0, field, pltpu.roll(field, 1, 1))
    half = pltpu.roll(field, 64, 1)
    before = jnp.where(row < 2, field, pltpu.roll(half, 2, 0))
    after = jnp.where(row >= ROWS - 2, field, pltpu.roll(half, ROWS - 2, 0))
    beside_y = half + jnp.where(lane < 64, before, after)
    return beside_x + (beside_y + (up + down)) - 6.0 * field


def kernel(
    n_space,
    biomass,
    resources,
    capacity,
    affinity,
    secretion,
    energy_yield,
    maintenance,
    motility,
    diffusivity,
    supply,
    growth_out,
    biomass_out,
    resources_out,
    seen,
    mass,
    cap_rows,
    aff_rows,
    flux,
    gain,
    consumed,
    product,
    net,
    relay_y,
    sum_y,
    reduced,
    relay_z,
    sum_z,
    final,
    halo_b,
    halo_r,
    send_sem,
    recv_sem,
):
    strains = biomass.shape[0]
    block = resources.shape[0]
    blocks = RING * RING
    half = block // 2
    me = lax.axis_index("species")
    place = lax.axis_index("space")
    y, h = lax.div(me, RING), lax.rem(me, RING)
    y_up, y_dn, y_op = (lax.rem(y + k, RING) for k in (1, 3, 2))
    h_up, h_dn, h_op = (lax.rem(h + k, RING) for k in (1, 3, 2))
    to_y_up = {"species": y_up * RING + h}
    to_y_dn = {"species": y_dn * RING + h}
    to_h_up = {"species": y * RING + h_up}
    to_h_dn = {"species": y * RING + h_dn}
    to_next = {"space": lax.rem(place + 1, n_space)}
    to_prev = {"space": lax.rem(place + n_space - 1, n_space)}

    barrier = pltpu.get_barrier_semaphore()
    for target in (to_h_up, to_h_dn, to_y_up, to_y_dn, to_next, to_prev):
        pl.semaphore_signal(barrier, inc=1, device_id=target, device_id_type=MESH)

    seen[me] = resources[...].astype(jnp.bfloat16)
    mass[...] = biomass[...].astype(jnp.float32)
    pad = jnp.zeros((LANES - strains, LANES), jnp.float32)
    cap_t = jnp.concatenate([capacity[...], pad], axis=0).T
    aff_t = jnp.concatenate([affinity[...], pad], axis=0).T
    for s in range(strains):
        cap_rows[s] = jnp.broadcast_to(cap_t[:, s : s + 1], (LANES, LANES))
        aff_rows[s] = jnp.broadcast_to(aff_t[:, s : s + 1], (LANES, LANES))
    sec_pad = jnp.zeros((LANES - strains, LANES), jnp.float32)
    sec = jnp.concatenate([secretion[...].astype(jnp.float32), sec_pad], axis=0).T
    sec = sec[:, :strains].astype(jnp.bfloat16)
    flux[...] = jnp.zeros_like(flux)
    gain[...] = jnp.zeros_like(gain)

    pl.semaphore_wait(barrier, 6)

    started = []

    def copy(index, src, dst, target):
        return pltpu.make_async_remote_copy(
            src_ref=src,
            dst_ref=dst,
            send_sem=send_sem.at[index],
            recv_sem=recv_sem.at[index],
            device_id=target,
            device_id_type=MESH,
        )

    def start(index, src, dst, target):
        c = copy(index, src, dst, target)
        c.start()
        started.append(c)

    def arrived(index, ref):
        copy(index, ref, ref, to_y_up).wait_recv()

    def whole(b):
        return seen.at[b]

    def low_half(b):
        return seen.at[b, pl.ds(0, half)]

    def high_half(b):
        return seen.at[b, pl.ds(half, half)]

    def at(yy, hh):
        return yy * RING + hh

    def y_send(column, hh):
        start(4 + 4 * column, whole(at(y, hh)), whole(at(y, hh)), to_y_up)
        start(5 + 4 * column, whole(at(y, hh)), whole(at(y, hh)), to_y_dn)

    def y_pass(column, hh):
        arrived(4 + 4 * column, whole(at(y_dn, hh)))
        part = low_half(at(y_dn, hh))
        start(6 + 4 * column, part, part, to_y_up)
        arrived(5 + 4 * column, whole(at(y_up, hh)))
        part = high_half(at(y_up, hh))
        start(7 + 4 * column, part, part, to_y_dn)

    def y_last(column, hh):
        arrived(6 + 4 * column, low_half(at(y_op, hh)))
        arrived(7 + 4 * column, high_half(at(y_op, hh)))

    def compute(b):
        xs = [seen[b, r].astype(jnp.float32) for r in range(block)]
        es = [energy_yield[b * block + r] for r in range(block)]

        def strain(s, sums):
            m = mass[s]
            f = flux[s]
            g = gain[s]
            out = []
            for r in range(block):
                row = pl.ds(b * block + r, 1)
                a = jnp.broadcast_to(aff_rows[s, row, :], (ROWS, LANES))
                c = jnp.broadcast_to(cap_rows[s, row, :], (ROWS, LANES))
                v = c / (a + xs[r])
                out.append(sums[r] + m * v)
                u = xs[r] * v
                f = f + u
                g = g + es[r] * u
            flux[s] = f
            gain[s] = g
            return tuple(out)

        zero = jnp.zeros((ROWS, LANES), jnp.float32)
        sums = lax.fori_loop(0, strains, strain, (zero,) * block)
        for r in range(block):
            consumed[pl.ds((b * block + r) * ROWS, ROWS), :] = sums[r] * xs[r]

    start(0, whole(me), whole(me), to_h_up)
    start(1, whole(me), whole(me), to_h_dn)
    y_send(0, h)
    compute(me)
    y_pass(0, h)
    compute(at(y_dn, h))
    compute(at(y_up, h))
    y_last(0, h)
    compute(at(y_op, h))
    arrived(0, whole(at(y, h_dn)))
    start(2, low_half(at(y, h_dn)), low_half(at(y, h_dn)), to_h_up)
    y_send(1, h_dn)
    arrived(1, whole(at(y, h_up)))
    start(3, high_half(at(y, h_up)), high_half(at(y, h_up)), to_h_dn)
    y_send(2, h_up)
    compute(at(y, h_dn))
    compute(at(y, h_up))
    y_pass(1, h_dn)
    y_pass(2, h_up)
    compute(at(y_dn, h_dn))
    compute(at(y_up, h_dn))
    compute(at(y_dn, h_up))
    compute(at(y_up, h_up))
    arrived(2, low_half(at(y, h_op)))
    part = low_half(at(y, h_op))
    start(16, part, part, to_y_up)
    start(17, part, part, to_y_dn)
    arrived(3, high_half(at(y, h_op)))
    part = high_half(at(y, h_op))
    start(18, part, part, to_y_up)
    start(19, part, part, to_y_dn)
    y_last(1, h_dn)
    y_last(2, h_up)
    compute(at(y_op, h_dn))
    compute(at(y_op, h_up))
    compute(at(y, h_op))
    arrived(16, low_half(at(y_dn, h_op)))
    start(20, low_half(at(y_dn, h_op)), low_half(at(y_dn, h_op)), to_y_up)
    arrived(19, high_half(at(y_up, h_op)))
    start(21, high_half(at(y_up, h_op)), high_half(at(y_up, h_op)), to_y_dn)
    start(22, biomass, halo_b.at[0], to_next)
    start(23, biomass, halo_b.at[1], to_prev)
    start(24, resources, halo_r.at[0], to_next)
    start(25, resources, halo_r.at[1], to_prev)
    arrived(18, high_half(at(y_dn, h_op)))
    compute(at(y_dn, h_op))
    arrived(17, low_half(at(y_up, h_op)))
    compute(at(y_up, h_op))
    arrived(20, low_half(at(y_op, h_op)))
    arrived(21, high_half(at(y_op, h_op)))
    compute(at(y_op, h_op))

    def to_product(s, _):
        value = (mass[s] * flux[s]).astype(jnp.bfloat16).astype(jnp.float32)
        product[pl.ds(s * ROWS, ROWS), :] = value
        return 0

    lax.fori_loop(0, strains, to_product, 0)

    rows = ROWS // PARTS
    first = rows // 2
    base = 26

    def lo(p):
        return pl.ds(p * rows, first)

    def hi(p):
        return pl.ds(p * rows + first, rows - first)

    def al(p):
        return pl.ds(p * rows, rows)

    def run(yy):
        return pl.ds(yy * RING, RING)

    for p in range(PARTS):
        for q in range(p * rows, (p + 1) * rows):
            made = product[pl.ds(q, strains, stride=ROWS), :].astype(jnp.bfloat16)
            secreted = jnp.dot(sec, made, preferred_element_type=jnp.float32)
            used = consumed[pl.ds(q, blocks * block, stride=ROWS), :]
            net[q] = (secreted - used).reshape(blocks, block, LANES)
        k = base + 8 * p
        start(k, net.at[lo(p), run(y_op)], relay_y.at[lo(p)], to_y_up)
        start(k + 1, net.at[hi(p), run(y_op)], relay_y.at[hi(p)], to_y_dn)

    for p in range(PARTS):
        k = base + 8 * p
        arrived(k, relay_y.at[lo(p)])
        net[lo(p), run(y_up)] = net[lo(p), run(y_up)] + relay_y[lo(p)]
        start(k + 2, net.at[al(p), run(y_up)], sum_y.at[0, al(p)], to_y_up)
        arrived(k + 1, relay_y.at[hi(p)])
        net[hi(p), run(y_dn)] = net[hi(p), run(y_dn)] + relay_y[hi(p)]
        start(k + 3, net.at[al(p), run(y_dn)], sum_y.at[1, al(p)], to_y_dn)

    arrived(22, halo_b.at[0])
    arrived(23, halo_b.at[1])

    def update(s, _):
        m = mass[s]
        grown = gain[s] - maintenance[s]
        low = halo_b[0, s].astype(jnp.float32)
        high = halo_b[1, s].astype(jnp.float32)
        growth_out[s] = grown
        spread = motility[s] * laplace(m, low, high)
        biomass_out[s] = m + TIME_STEP * (m * grown + spread)
        return 0

    lax.fori_loop(0, strains, update, 0)

    for p in range(PARTS):
        k = base + 8 * p
        arrived(k + 2, sum_y.at[0, al(p)])
        arrived(k + 3, sum_y.at[1, al(p)])
        reduced[al(p)] = net[al(p), run(y)] + (sum_y[0, al(p)] + sum_y[1, al(p)])
        start(k + 4, reduced.at[lo(p), h_op], relay_z.at[lo(p)], to_h_up)
        start(k + 5, reduced.at[hi(p), h_op], relay_z.at[hi(p)], to_h_dn)

    for p in range(PARTS):
        k = base + 8 * p
        arrived(k + 4, relay_z.at[lo(p)])
        reduced[lo(p), h_up] = reduced[lo(p), h_up] + relay_z[lo(p)]
        start(k + 6, reduced.at[al(p), h_up], sum_z.at[0, al(p)], to_h_up)
        arrived(k + 5, relay_z.at[hi(p)])
        reduced[hi(p), h_dn] = reduced[hi(p), h_dn] + relay_z[hi(p)]
        start(k + 7, reduced.at[al(p), h_dn], sum_z.at[1, al(p)], to_h_dn)

    arrived(24, halo_r.at[0])
    arrived(25, halo_r.at[1])
    for p in range(PARTS):
        k = base + 8 * p
        arrived(k + 6, sum_z.at[0, al(p)])
        arrived(k + 7, sum_z.at[1, al(p)])
        for q in range(p * rows, (p + 1) * rows):
            total = reduced[q, h] + (sum_z[0, q] + sum_z[1, q])
            final[pl.ds(q, block, stride=ROWS), :] = total
    for r in range(block):
        value = resources[r]
        spread = diffusivity[r] * laplace(value, halo_r[0, r], halo_r[1, r])
        released = final[pl.ds(r * ROWS, ROWS), :]
        resources_out[r] = value + TIME_STEP * (spread + released + supply[r])

    for c in started:
        c.wait_send()


def per_device(
    biomass,
    resources,
    capacity,
    affinity,
    secretion,
    energy_yield,
    maintenance,
    motility,
    diffusivity,
    supply,
    n_space,
):
    strains, slab, plane = biomass.shape
    block = resources.shape[0]
    blocks = RING * RING
    tiles = plane // LANES

    def split(field):
        parts = field.reshape(field.shape[0], slab, tiles, LANES)
        return parts.transpose(0, 2, 1, 3).reshape(field.shape[0], ROWS, LANES)

    def join(field):
        parts = field.reshape(field.shape[0], tiles, slab, LANES)
        return parts.transpose(0, 2, 1, 3).reshape(field.shape[0], slab, plane)

    f32 = jnp.float32
    vmem = pl.BlockSpec(memory_space=pltpu.VMEM)
    smem = pl.BlockSpec(memory_space=pltpu.SMEM)
    copies = 26 + 8 * PARTS
    outs = pl.pallas_call(
        functools.partial(kernel, n_space),
        out_shape=(
            jax.ShapeDtypeStruct((strains, ROWS, LANES), f32),
            jax.ShapeDtypeStruct((strains, ROWS, LANES), f32),
            jax.ShapeDtypeStruct((block, ROWS, LANES), f32),
        ),
        in_specs=[vmem] * 5 + [smem] * 5,
        out_specs=(vmem,) * 3,
        scratch_shapes=[
            pltpu.VMEM((blocks, block, ROWS, LANES), jnp.bfloat16),
            pltpu.VMEM((strains, ROWS, LANES), f32),
            pltpu.VMEM((strains, LANES, LANES), f32),
            pltpu.VMEM((strains, LANES, LANES), f32),
            pltpu.VMEM((strains, ROWS, LANES), f32),
            pltpu.VMEM((strains, ROWS, LANES), f32),
            pltpu.VMEM((blocks * block * ROWS, LANES), f32),
            pltpu.VMEM((strains * ROWS, LANES), f32),
            pltpu.VMEM((ROWS, blocks, block, LANES), f32),
            pltpu.VMEM((ROWS, RING, block, LANES), f32),
            pltpu.VMEM((2, ROWS, RING, block, LANES), f32),
            pltpu.VMEM((ROWS, RING, block, LANES), f32),
            pltpu.VMEM((ROWS, block, LANES), f32),
            pltpu.VMEM((2, ROWS, block, LANES), f32),
            pltpu.VMEM((block * ROWS, LANES), f32),
            pltpu.VMEM((2, strains, ROWS, LANES), jnp.bfloat16),
            pltpu.VMEM((2, block, ROWS, LANES), f32),
            pltpu.SemaphoreType.DMA((copies,)),
            pltpu.SemaphoreType.DMA((copies,)),
        ],
        compiler_params=pltpu.CompilerParams(
            collective_id=0, has_side_effects=True, vmem_limit_bytes=32 << 20
        ),
    )(
        split(biomass),
        split(resources),
        capacity,
        affinity,
        secretion.T,
        energy_yield,
        maintenance,
        motility,
        diffusivity,
        supply,
    )
    return tuple(join(out) for out in outs)


def solution(mesh):
    return jax.shard_map(
        functools.partial(per_device, n_space=mesh.shape["space"]),
        mesh=mesh,
        in_specs=(
            P("species", "space", None),
            P("species", "space", None),
            P("species", None),
            P("species", None),
            P(None, "species"),
            P(),
            P("species"),
            P("species"),
            P("species"),
            P("species"),
        ),
        out_specs=(
            P("species", "space", None),
            P("species", "space", None),
            P("species", "space", None),
        ),
        check_vma=False,
    )
```

```python
import functools

import jax
import jax.numpy as jnp
from jax import lax
from jax.experimental import pallas as pl
from jax.experimental.pallas import tpu as pltpu
from jax.sharding import PartitionSpec as P

MESH = pl.DeviceIdType.MESH
RING = 4
GROUP = 4
UNROLL = 8
PARTS = 4
TIME_STEP = 0.25
SMALL = 2.0**-6
STEPS = 19.5
BOTTOM = 125.0
ROWS = 16
LANES = 128


def laplace(field, low, high):
    row = lax.broadcasted_iota(jnp.int32, (ROWS, LANES), 0)
    lane = lax.broadcasted_iota(jnp.int32, (ROWS, LANES), 1)
    odd = lax.rem(row, 2) == 1
    z = lax.rem(lane, 64)
    both = field + jnp.where(odd, low, high)
    beside_x = jnp.where(odd, pltpu.roll(both, 1, 0), pltpu.roll(both, ROWS - 1, 0))
    up = jnp.where(z == 63, field, pltpu.roll(field, LANES - 1, 1))
    down = jnp.where(z == 0, field, pltpu.roll(field, 1, 1))
    half = pltpu.roll(field, 64, 1)
    before = jnp.where(row < 2, field, pltpu.roll(half, 2, 0))
    after = jnp.where(row >= ROWS - 2, field, pltpu.roll(half, ROWS - 2, 0))
    beside_y = half + jnp.where(lane < 64, before, after)
    return beside_x + (beside_y + (up + down)) - 6.0 * field


def encode(value):
    level = jnp.log2(jnp.abs(value) * (1.0 / SMALL) + 1.0)
    code = jnp.exp2(level * STEPS - BOTTOM)
    return jnp.where(value < 0.0, -code, code).astype(jnp.bfloat16)


def decode(code):
    code = code.astype(jnp.float32)
    level = (jnp.log2(jnp.abs(code)) + BOTTOM) * (1.0 / STEPS)
    value = jnp.exp2(level) * SMALL - SMALL
    return jnp.where(code < 0.0, -value, value)


def kernel(
    n_space,
    biomass_in,
    resources_in,
    capacity_in,
    affinity_in,
    secretion_in,
    energy_yield_in,
    maintenance_in,
    motility_in,
    diffusivity_in,
    supply_in,
    growth_hbm,
    biomass_hbm,
    resources_hbm,
    biomass,
    resources,
    capacity,
    affinity,
    secretion,
    energy_yield,
    maintenance,
    motility,
    diffusivity,
    supply,
    seen,
    mass,
    cap_rows,
    aff_rows,
    flux,
    gain,
    consumed,
    product,
    net,
    pass_y,
    relay_y,
    send_y,
    sum_y,
    reduced,
    pass_z,
    relay_z,
    send_z,
    sum_z,
    final,
    halo_b,
    halo_r,
    send_sem,
    recv_sem,
    load_sem,
    store_sem,
    growth_out,
    biomass_out,
    resources_out,
):
    strains = biomass.shape[0]
    block = resources.shape[0]
    blocks = RING * RING
    half = block // 2
    me = lax.axis_index("species")
    place = lax.axis_index("space")
    y, h = lax.div(me, RING), lax.rem(me, RING)
    y_up, y_dn, y_op = (lax.rem(y + k, RING) for k in (1, 3, 2))
    h_up, h_dn, h_op = (lax.rem(h + k, RING) for k in (1, 3, 2))
    to_y_up = {"species": y_up * RING + h}
    to_y_dn = {"species": y_dn * RING + h}
    to_h_up = {"species": y * RING + h_up}
    to_h_dn = {"species": y * RING + h_dn}
    to_next = {"space": lax.rem(place + 1, n_space)}
    to_prev = {"space": lax.rem(place + n_space - 1, n_space)}

    barrier = pltpu.get_barrier_semaphore()
    for target in (to_h_up, to_h_dn, to_y_up, to_y_dn, to_next, to_prev):
        pl.semaphore_signal(barrier, inc=1, device_id=target, device_id_type=MESH)

    pairs = (
        (resources_in, resources),
        (biomass_in, biomass),
        (capacity_in, capacity),
        (affinity_in, affinity),
        (secretion_in, secretion),
        (energy_yield_in, energy_yield),
        (maintenance_in, maintenance),
        (motility_in, motility),
        (diffusivity_in, diffusivity),
        (supply_in, supply),
    )
    loads = [
        pltpu.make_async_copy(src, dst, load_sem.at[i])
        for i, (src, dst) in enumerate(pairs)
    ]
    for load in loads:
        load.start()
    loads[0].wait()
    seen[me] = resources[...].astype(jnp.bfloat16)

    pl.semaphore_wait(barrier, 6)

    started = []

    def copy(index, src, dst, target):
        return pltpu.make_async_remote_copy(
            src_ref=src,
            dst_ref=dst,
            send_sem=send_sem.at[index],
            recv_sem=recv_sem.at[index],
            device_id=target,
            device_id_type=MESH,
        )

    def start(index, src, dst, target):
        c = copy(index, src, dst, target)
        c.start()
        started.append(c)

    def arrived(index, ref):
        copy(index, ref, ref, to_y_up).wait_recv()

    def whole(b):
        return seen.at[b]

    def low_half(b):
        return seen.at[b, pl.ds(0, half)]

    def high_half(b):
        return seen.at[b, pl.ds(half, half)]

    def at(yy, hh):
        return yy * RING + hh

    def y_send(column, hh):
        start(4 + 4 * column, whole(at(y, hh)), whole(at(y, hh)), to_y_up)
        start(5 + 4 * column, whole(at(y, hh)), whole(at(y, hh)), to_y_dn)

    def y_pass(column, hh):
        arrived(4 + 4 * column, whole(at(y_dn, hh)))
        part = low_half(at(y_dn, hh))
        start(6 + 4 * column, part, part, to_y_up)
        arrived(5 + 4 * column, whole(at(y_up, hh)))
        part = high_half(at(y_up, hh))
        start(7 + 4 * column, part, part, to_y_dn)

    def y_last(column, hh):
        arrived(6 + 4 * column, low_half(at(y_op, hh)))
        arrived(7 + 4 * column, high_half(at(y_op, hh)))

    def compute(b):
        def quarter(part, _):
            first_r = part * GROUP
            xs = [seen[b, first_r + r].astype(jnp.float32) for r in range(GROUP)]
            es = [energy_yield[b * block + first_r + r] for r in range(GROUP)]

            def strain(i, sums):
                sums = list(sums)
                for k in range(UNROLL):
                    s = i * UNROLL + k
                    m = mass[s]
                    f = flux[s]
                    g = gain[s]
                    for r in range(GROUP):
                        row = pl.ds(b * block + first_r + r, 1)
                        a = jnp.broadcast_to(aff_rows[s, row, :], (ROWS, LANES))
                        c = jnp.broadcast_to(cap_rows[s, row, :], (ROWS, LANES))
                        v = c / (a + xs[r])
                        sums[r] = sums[r] + m * v
                        u = xs[r] * v
                        f = f + u
                        g = g + es[r] * u
                    flux[s] = f
                    gain[s] = g
                return tuple(sums)

            zero = jnp.zeros((ROWS, LANES), jnp.float32)
            sums = lax.fori_loop(0, strains // UNROLL, strain, (zero,) * GROUP)
            for r in range(GROUP):
                row = pl.multiple_of((b * block + first_r + r) * ROWS, ROWS)
                consumed[pl.ds(row, ROWS), :] = sums[r] * xs[r]
            return 0

        lax.fori_loop(0, block // GROUP, quarter, 0)

    start(0, low_half(me), low_half(me), to_h_up)
    start(3, high_half(me), high_half(me), to_h_dn)
    start(1, high_half(me), high_half(me), to_h_up)
    start(2, low_half(me), low_half(me), to_h_dn)
    y_send(0, h)

    for load in loads[1:]:
        load.wait()
    mass[...] = biomass[...].astype(jnp.float32)
    pad = jnp.zeros((LANES - strains, LANES), jnp.float32)
    cap_t = jnp.concatenate([capacity[...], pad], axis=0).T
    aff_t = jnp.concatenate([affinity[...], pad], axis=0).T
    for s in range(strains):
        cap_rows[s] = jnp.broadcast_to(cap_t[:, s : s + 1], (LANES, LANES))
        aff_rows[s] = jnp.broadcast_to(aff_t[:, s : s + 1], (LANES, LANES))
    sec = jnp.concatenate([secretion[...].astype(jnp.float32), pad], axis=0).T
    sec = sec[:, :strains].astype(jnp.bfloat16)
    flux[...] = jnp.zeros_like(flux)
    gain[...] = jnp.zeros_like(gain)

    compute(me)
    y_pass(0, h)
    compute(at(y_dn, h))
    compute(at(y_up, h))
    y_last(0, h)
    compute(at(y_op, h))
    arrived(0, low_half(at(y, h_dn)))
    start(22, low_half(at(y, h_dn)), low_half(at(y, h_dn)), to_h_up)
    arrived(3, high_half(at(y, h_up)))
    start(23, high_half(at(y, h_up)), high_half(at(y, h_up)), to_h_dn)
    arrived(1, high_half(at(y, h_dn)))
    y_send(1, h_dn)
    arrived(2, low_half(at(y, h_up)))
    y_send(2, h_up)
    compute(at(y, h_dn))
    compute(at(y, h_up))
    y_pass(1, h_dn)
    y_pass(2, h_up)
    compute(at(y_dn, h_dn))
    compute(at(y_up, h_dn))
    compute(at(y_dn, h_up))
    compute(at(y_up, h_up))
    arrived(22, low_half(at(y, h_op)))
    part = low_half(at(y, h_op))
    start(16, part, part, to_y_up)
    start(17, part, part, to_y_dn)
    arrived(23, high_half(at(y, h_op)))
    part = high_half(at(y, h_op))
    start(18, part, part, to_y_up)
    start(19, part, part, to_y_dn)
    y_last(1, h_dn)
    y_last(2, h_up)
    compute(at(y_op, h_dn))
    compute(at(y_op, h_up))
    compute(at(y, h_op))
    arrived(16, low_half(at(y_dn, h_op)))
    start(20, low_half(at(y_dn, h_op)), low_half(at(y_dn, h_op)), to_y_up)
    arrived(19, high_half(at(y_up, h_op)))
    start(21, high_half(at(y_up, h_op)), high_half(at(y_up, h_op)), to_y_dn)
    start(24, biomass, halo_b.at[0], to_next)
    start(25, biomass, halo_b.at[1], to_prev)
    start(26, resources, halo_r.at[0], to_next)
    start(27, resources, halo_r.at[1], to_prev)
    arrived(18, high_half(at(y_dn, h_op)))
    compute(at(y_dn, h_op))
    arrived(17, low_half(at(y_up, h_op)))
    compute(at(y_up, h_op))
    arrived(20, low_half(at(y_op, h_op)))
    arrived(21, high_half(at(y_op, h_op)))
    compute(at(y_op, h_op))

    def to_product(s, _):
        value = (mass[s] * flux[s]).astype(jnp.bfloat16).astype(jnp.float32)
        product[pl.ds(pl.multiple_of(s * ROWS, ROWS), ROWS), :] = value
        return 0

    lax.fori_loop(0, strains, to_product, 0, unroll=4)

    rows = ROWS // PARTS
    first = rows // 2
    base = 28
    span = RING * block

    def lows(p):
        return range(p * rows, p * rows + first)

    def highs(p):
        return range(p * rows + first, (p + 1) * rows)

    def both(p):
        return range(p * rows, (p + 1) * rows)

    def of(rng):
        return pl.ds(rng.start, len(rng))

    def pairs_of(rng):
        return range(rng.start // 2, rng.stop // 2)

    def run(yy):
        return pl.ds(pl.multiple_of(yy * span, span), span)

    def pair(k, hh):
        at_h = pl.ds(pl.multiple_of(hh * block, block), block)
        return jnp.concatenate([reduced[2 * k, at_h], reduced[2 * k + 1, at_h]], axis=0)

    for p in range(PARTS):
        for q in both(p):
            made = product[pl.ds(q, strains, stride=ROWS), :].astype(jnp.bfloat16)
            secreted = jnp.dot(sec, made, preferred_element_type=jnp.float32)
            used = consumed[pl.ds(q, blocks * block, stride=ROWS), :]
            net[q] = secreted - used
            pass_y[q] = encode(net[q, run(y_op)])
        k = base + 8 * p
        start(k, pass_y.at[of(lows(p))], relay_y.at[of(lows(p))], to_y_up)
        start(k + 1, pass_y.at[of(highs(p))], relay_y.at[of(highs(p))], to_y_dn)

    for p in range(PARTS):
        k = base + 8 * p
        for q in highs(p):
            send_y[0, q] = encode(net[q, run(y_up)])
        for q in lows(p):
            send_y[1, q] = encode(net[q, run(y_dn)])
        arrived(k, relay_y.at[of(lows(p))])
        for q in lows(p):
            send_y[0, q] = encode(net[q, run(y_up)] + decode(relay_y[q]))
        start(k + 2, send_y.at[0, of(both(p))], sum_y.at[0, of(both(p))], to_y_up)
        arrived(k + 1, relay_y.at[of(highs(p))])
        for q in highs(p):
            send_y[1, q] = encode(net[q, run(y_dn)] + decode(relay_y[q]))
        start(k + 3, send_y.at[1, of(both(p))], sum_y.at[1, of(both(p))], to_y_dn)

    arrived(24, halo_b.at[0])
    arrived(25, halo_b.at[1])

    def update(s, _):
        m = mass[s]
        grown = gain[s] - maintenance[s]
        low = halo_b[0, s].astype(jnp.float32)
        high = halo_b[1, s].astype(jnp.float32)
        growth_out[s] = grown
        spread = motility[s] * laplace(m, low, high)
        biomass_out[s] = m + TIME_STEP * (m * grown + spread)
        return 0

    lax.fori_loop(0, strains, update, 0, unroll=2)
    stores = [
        pltpu.make_async_copy(growth_out, growth_hbm, store_sem.at[0]),
        pltpu.make_async_copy(biomass_out, biomass_hbm, store_sem.at[1]),
        pltpu.make_async_copy(resources_out, resources_hbm, store_sem.at[2]),
    ]
    stores[0].start()
    stores[1].start()

    for p in range(PARTS):
        k = base + 8 * p
        arrived(k + 2, sum_y.at[0, of(both(p))])
        arrived(k + 3, sum_y.at[1, of(both(p))])
        for q in both(p):
            others = decode(sum_y[0, q]) + decode(sum_y[1, q])
            reduced[q] = net[q, run(y)] + others
        for j in pairs_of(both(p)):
            pass_z[j] = encode(pair(j, h_op))
        low, high = of(pairs_of(lows(p))), of(pairs_of(highs(p)))
        start(k + 4, pass_z.at[low], relay_z.at[low], to_h_up)
        start(k + 5, pass_z.at[high], relay_z.at[high], to_h_dn)

    for p in range(PARTS):
        k = base + 8 * p
        low, high = pairs_of(lows(p)), pairs_of(highs(p))
        every = of(pairs_of(both(p)))
        for j in high:
            send_z[0, j] = encode(pair(j, h_up))
        for j in low:
            send_z[1, j] = encode(pair(j, h_dn))
        arrived(k + 4, relay_z.at[of(low)])
        for j in low:
            send_z[0, j] = encode(pair(j, h_up) + decode(relay_z[j]))
        start(k + 6, send_z.at[0, every], sum_z.at[0, every], to_h_up)
        arrived(k + 5, relay_z.at[of(high)])
        for j in high:
            send_z[1, j] = encode(pair(j, h_dn) + decode(relay_z[j]))
        start(k + 7, send_z.at[1, every], sum_z.at[1, every], to_h_dn)

    arrived(26, halo_r.at[0])
    arrived(27, halo_r.at[1])
    for r in range(block):
        value = resources[r]
        spread = diffusivity[r] * laplace(value, halo_r[0, r], halo_r[1, r])
        resources_out[r] = value + TIME_STEP * (spread + supply[r])
    for p in range(PARTS):
        k = base + 8 * p
        arrived(k + 6, sum_z.at[0, of(pairs_of(both(p)))])
        arrived(k + 7, sum_z.at[1, of(pairs_of(both(p)))])
        for j in pairs_of(both(p)):
            total = pair(j, h) + (decode(sum_z[0, j]) + decode(sum_z[1, j]))
            final[pl.ds(2 * j, block, stride=ROWS), :] = total[:block]
            final[pl.ds(2 * j + 1, block, stride=ROWS), :] = total[block:]
    for r in range(block):
        released = final[pl.ds(r * ROWS, ROWS), :]
        resources_out[r] = resources_out[r] + TIME_STEP * released
    stores[2].start()
    for c in started:
        c.wait_send()
    for store in stores:
        store.wait()


def store_kernel(a, b, c, a_out, b_out, c_out, a_mid, b_mid, c_mid, sem):
    chains = ((a, a_mid, a_out), (b, b_mid, b_out), (c, c_mid, c_out))
    loads = []
    stores = []
    for i, (src, mid, dst) in enumerate(chains):
        loads.append(pltpu.make_async_copy(src, mid, sem.at[0, i]))
        stores.append(pltpu.make_async_copy(mid, dst, sem.at[1, i]))
    for load in loads:
        load.start()
    for load, store in zip(loads, stores):
        load.wait()
        store.start()
    for store in stores:
        store.wait()


def per_device(
    biomass,
    resources,
    capacity,
    affinity,
    secretion,
    energy_yield,
    maintenance,
    motility,
    diffusivity,
    supply,
    n_space,
):
    strains, slab, plane = biomass.shape
    block = resources.shape[0]
    blocks = RING * RING
    tiles = plane // LANES

    def split(field):
        parts = field.reshape(field.shape[0], slab, tiles, LANES)
        return parts.transpose(0, 2, 1, 3).reshape(field.shape[0], ROWS, LANES)

    def join(field):
        parts = field.reshape(field.shape[0], tiles, slab, LANES)
        return parts.transpose(0, 2, 1, 3).reshape(field.shape[0], slab, plane)

    f32, bf16 = jnp.float32, jnp.bfloat16
    hbm = pl.BlockSpec(memory_space=pltpu.HBM)
    copies = 28 + 8 * PARTS
    outs = pl.pallas_call(
        functools.partial(kernel, n_space),
        out_shape=(
            jax.ShapeDtypeStruct((strains, ROWS, LANES), f32),
            jax.ShapeDtypeStruct((strains, ROWS, LANES), f32),
            jax.ShapeDtypeStruct((block, ROWS, LANES), f32),
        ),
        in_specs=[hbm] * 10,
        out_specs=(hbm,) * 3,
        scratch_shapes=[
            pltpu.VMEM((strains, ROWS, LANES), jnp.bfloat16),
            pltpu.VMEM((block, ROWS, LANES), f32),
            pltpu.VMEM(capacity.shape, f32),
            pltpu.VMEM(affinity.shape, f32),
            pltpu.VMEM((strains, blocks * block), jnp.bfloat16),
            pltpu.SMEM(energy_yield.shape, f32),
            pltpu.SMEM(maintenance.shape, f32),
            pltpu.SMEM(motility.shape, f32),
            pltpu.SMEM(diffusivity.shape, f32),
            pltpu.SMEM(supply.shape, f32),
            pltpu.VMEM((blocks, block, ROWS, LANES), jnp.bfloat16),
            pltpu.VMEM((strains, ROWS, LANES), f32),
            pltpu.VMEM((strains, LANES, LANES), f32),
            pltpu.VMEM((strains, LANES, LANES), f32),
            pltpu.VMEM((strains, ROWS, LANES), f32),
            pltpu.VMEM((strains, ROWS, LANES), f32),
            pltpu.VMEM((blocks * block * ROWS, LANES), f32),
            pltpu.VMEM((strains * ROWS, LANES), f32),
            pltpu.VMEM((ROWS, blocks * block, LANES), f32),
            pltpu.VMEM((ROWS, RING * block, LANES), bf16),
            pltpu.VMEM((ROWS, RING * block, LANES), bf16),
            pltpu.VMEM((2, ROWS, RING * block, LANES), bf16),
            pltpu.VMEM((2, ROWS, RING * block, LANES), bf16),
            pltpu.VMEM((ROWS, RING * block, LANES), f32),
            pltpu.VMEM((ROWS // 2, 2 * block, LANES), bf16),
            pltpu.VMEM((ROWS // 2, 2 * block, LANES), bf16),
            pltpu.VMEM((2, ROWS // 2, 2 * block, LANES), bf16),
            pltpu.VMEM((2, ROWS // 2, 2 * block, LANES), bf16),
            pltpu.VMEM((block * ROWS, LANES), f32),
            pltpu.VMEM((2, strains, ROWS, LANES), jnp.bfloat16),
            pltpu.VMEM((2, block, ROWS, LANES), f32),
            pltpu.SemaphoreType.DMA((copies,)),
            pltpu.SemaphoreType.DMA((copies,)),
            pltpu.SemaphoreType.DMA((10,)),
            pltpu.SemaphoreType.DMA((3,)),
            pltpu.VMEM((strains, ROWS, LANES), f32),
            pltpu.VMEM((strains, ROWS, LANES), f32),
            pltpu.VMEM((block, ROWS, LANES), f32),
        ],
        compiler_params=pltpu.CompilerParams(
            collective_id=0, has_side_effects=True, vmem_limit_bytes=67043328
        ),
    )(
        split(biomass),
        split(resources),
        capacity,
        affinity,
        secretion.T,
        energy_yield,
        maintenance,
        motility,
        diffusivity,
        supply,
    )
    outs = pl.pallas_call(
        store_kernel,
        out_shape=tuple(jax.ShapeDtypeStruct(out.shape, f32) for out in outs),
        in_specs=[hbm] * 3,
        out_specs=(hbm,) * 3,
        scratch_shapes=[
            *(pltpu.VMEM(out.shape, f32) for out in outs),
            pltpu.SemaphoreType.DMA((2, 3)),
        ],
        compiler_params=pltpu.CompilerParams(vmem_limit_bytes=67043328),
    )(*outs)
    return tuple(join(out) for out in outs)


def solution(mesh):
    return jax.shard_map(
        functools.partial(per_device, n_space=mesh.shape["space"]),
        mesh=mesh,
        in_specs=(
            P("species", "space", None),
            P("species", "space", None),
            P("species", None),
            P("species", None),
            P(None, "species"),
            P(),
            P("species"),
            P("species"),
            P("species"),
            P("species"),
        ),
        out_specs=(
            P("species", "space", None),
            P("species", "space", None),
            P("species", "space", None),
        ),
        check_vma=False,
    )
```

```python
import functools

import jax
import jax.numpy as jnp
from jax import lax
from jax.experimental import pallas as pl
from jax.experimental.pallas import tpu as pltpu
from jax.sharding import PartitionSpec as P

MESH = pl.DeviceIdType.MESH
RING = 4
GROUP = 4
UNROLL = 16
PARTS = 2
TIME_STEP = 0.25
SMALL = 2.0**-6
STEPS = 19.5
BOTTOM = 125.0
ROWS = 16
LANES = 128


def laplace(field, low, high):
    row = lax.broadcasted_iota(jnp.int32, (ROWS, LANES), 0)
    lane = lax.broadcasted_iota(jnp.int32, (ROWS, LANES), 1)
    odd = lax.rem(row, 2) == 1
    z = lax.rem(lane, 64)
    both = field + jnp.where(odd, low, high)
    beside_x = jnp.where(odd, pltpu.roll(both, 1, 0), pltpu.roll(both, ROWS - 1, 0))
    up = jnp.where(z == 63, field, pltpu.roll(field, LANES - 1, 1))
    down = jnp.where(z == 0, field, pltpu.roll(field, 1, 1))
    half = pltpu.roll(field, 64, 1)
    before = jnp.where(row < 2, field, pltpu.roll(half, 2, 0))
    after = jnp.where(row >= ROWS - 2, field, pltpu.roll(half, ROWS - 2, 0))
    beside_y = half + jnp.where(lane < 64, before, after)
    return beside_x + (beside_y + (up + down)) - 6.0 * field


def encode(value):
    level = jnp.log2(jnp.abs(value) * (1.0 / SMALL) + 1.0)
    code = jnp.exp2(level * STEPS - BOTTOM)
    return jnp.where(value < 0.0, -code, code).astype(jnp.bfloat16)


def decode(code):
    code = code.astype(jnp.float32)
    level = (jnp.log2(jnp.abs(code)) + BOTTOM) * (1.0 / STEPS)
    value = jnp.exp2(level) * SMALL - SMALL
    return jnp.where(code < 0.0, -value, value)


def kernel(
    n_space,
    biomass_in,
    resources_in,
    capacity_in,
    affinity_in,
    secretion_in,
    energy_yield_in,
    maintenance_in,
    motility_in,
    diffusivity_in,
    supply_in,
    growth_hbm,
    biomass_hbm,
    resources_hbm,
    biomass,
    resources,
    capacity,
    affinity,
    secretion,
    energy_yield,
    maintenance,
    motility,
    diffusivity,
    supply,
    seen,
    mass,
    cap_rows,
    aff_rows,
    flux,
    gain,
    consumed,
    product,
    net,
    send_y,
    sum_y,
    reduced,
    send_z,
    sum_z,
    final,
    halo_b,
    halo_r,
    send_sem,
    recv_sem,
    load_sem,
    store_sem,
    growth_out,
    biomass_out,
    resources_out,
):
    strains = biomass.shape[0]
    block = resources.shape[0]
    blocks = RING * RING
    half = block // 2
    me = lax.axis_index("species")
    place = lax.axis_index("space")
    y, h = lax.div(me, RING), lax.rem(me, RING)
    y_up, y_dn, y_op = (lax.rem(y + k, RING) for k in (1, 3, 2))
    h_up, h_dn, h_op = (lax.rem(h + k, RING) for k in (1, 3, 2))
    to_y_up = {"species": y_up * RING + h}
    to_y_dn = {"species": y_dn * RING + h}
    to_y_op = {"species": y_op * RING + h}
    to_h_up = {"species": y * RING + h_up}
    to_h_dn = {"species": y * RING + h_dn}
    to_h_op = {"species": y * RING + h_op}
    to_next = {"space": lax.rem(place + 1, n_space)}
    to_prev = {"space": lax.rem(place + n_space - 1, n_space)}

    barrier = pltpu.get_barrier_semaphore()
    for target in (to_h_up, to_h_dn, to_y_up, to_y_dn, to_y_op, to_next, to_prev):
        pl.semaphore_signal(barrier, inc=1, device_id=target, device_id_type=MESH)

    pairs = (
        (resources_in, resources),
        (biomass_in, biomass),
        (capacity_in, capacity),
        (affinity_in, affinity),
        (secretion_in, secretion),
        (energy_yield_in, energy_yield),
        (maintenance_in, maintenance),
        (motility_in, motility),
        (diffusivity_in, diffusivity),
        (supply_in, supply),
    )
    loads = [
        pltpu.make_async_copy(src, dst, load_sem.at[i])
        for i, (src, dst) in enumerate(pairs)
    ]
    for load in loads:
        load.start()
    loads[0].wait()
    seen[me] = resources[...].astype(jnp.bfloat16)

    pl.semaphore_wait(barrier, 7)

    started = []

    def copy(index, src, dst, target):
        return pltpu.make_async_remote_copy(
            src_ref=src,
            dst_ref=dst,
            send_sem=send_sem.at[index],
            recv_sem=recv_sem.at[index],
            device_id=target,
            device_id_type=MESH,
        )

    def start(index, src, dst, target):
        c = copy(index, src, dst, target)
        c.start()
        started.append(c)

    def arrived(index, ref):
        copy(index, ref, ref, to_y_up).wait_recv()

    def whole(b):
        return seen.at[b]

    def low_half(b):
        return seen.at[b, pl.ds(0, half)]

    def high_half(b):
        return seen.at[b, pl.ds(half, half)]

    def at(yy, hh):
        return yy * RING + hh

    def y_send(column, part):
        start(6 + 3 * column, part, part, to_y_up)
        start(7 + 3 * column, part, part, to_y_dn)
        start(8 + 3 * column, part, part, to_y_op)

    def from_dn(column, part):
        arrived(6 + 3 * column, part)

    def from_up(column, part):
        arrived(7 + 3 * column, part)

    def from_op(column, part):
        arrived(8 + 3 * column, part)

    def compute(b):
        def quarter(part, _):
            first_r = part * GROUP
            xs = [seen[b, first_r + r].astype(jnp.float32) for r in range(GROUP)]
            es = [energy_yield[b * block + first_r + r] for r in range(GROUP)]

            def strain(i, sums):
                sums = list(sums)
                for k in range(UNROLL):
                    s = i * UNROLL + k
                    m = mass[s]
                    f = flux[s]
                    g = gain[s]
                    for r in range(GROUP):
                        row = pl.ds(b * block + first_r + r, 1)
                        a = jnp.broadcast_to(aff_rows[s, row, :], (ROWS, LANES))
                        c = jnp.broadcast_to(cap_rows[s, row, :], (ROWS, LANES))
                        v = c / (a + xs[r])
                        sums[r] = sums[r] + m * v
                        u = xs[r] * v
                        f = f + u
                        g = g + es[r] * u
                    flux[s] = f
                    gain[s] = g
                return tuple(sums)

            zero = jnp.zeros((ROWS, LANES), jnp.float32)
            sums = lax.fori_loop(0, strains // UNROLL, strain, (zero,) * GROUP)
            for r in range(GROUP):
                row = pl.multiple_of((b * block + first_r + r) * ROWS, ROWS)
                consumed[pl.ds(row, ROWS), :] = sums[r] * xs[r]
            return 0

        lax.fori_loop(0, block // GROUP, quarter, 0)

    start(0, low_half(me), low_half(me), to_h_up)
    start(3, high_half(me), high_half(me), to_h_dn)
    start(1, high_half(me), high_half(me), to_h_up)
    start(2, low_half(me), low_half(me), to_h_dn)
    y_send(0, whole(me))

    for load in loads[1:]:
        load.wait()
    mass[...] = biomass[...].astype(jnp.float32)
    pad = jnp.zeros((LANES - strains, LANES), jnp.float32)
    cap_t = jnp.concatenate([capacity[...], pad], axis=0).T
    aff_t = jnp.concatenate([affinity[...], pad], axis=0).T
    for s in range(strains):
        cap_rows[s] = jnp.broadcast_to(cap_t[:, s : s + 1], (LANES, LANES))
        aff_rows[s] = jnp.broadcast_to(aff_t[:, s : s + 1], (LANES, LANES))
    sec = jnp.concatenate([secretion[...].astype(jnp.float32), pad], axis=0).T
    sec = sec[:, :strains].astype(jnp.bfloat16)
    flux[...] = jnp.zeros_like(flux)
    gain[...] = jnp.zeros_like(gain)

    compute(me)
    from_dn(0, whole(at(y_dn, h)))
    compute(at(y_dn, h))
    from_up(0, whole(at(y_up, h)))
    compute(at(y_up, h))
    arrived(0, low_half(at(y, h_dn)))
    start(4, low_half(at(y, h_dn)), low_half(at(y, h_dn)), to_h_up)
    arrived(3, high_half(at(y, h_up)))
    start(5, high_half(at(y, h_up)), high_half(at(y, h_up)), to_h_dn)
    arrived(1, high_half(at(y, h_dn)))
    y_send(1, whole(at(y, h_dn)))
    arrived(2, low_half(at(y, h_up)))
    y_send(2, whole(at(y, h_up)))
    from_op(0, whole(at(y_op, h)))
    compute(at(y_op, h))
    compute(at(y, h_dn))
    compute(at(y, h_up))
    from_dn(1, whole(at(y_dn, h_dn)))
    compute(at(y_dn, h_dn))
    from_up(1, whole(at(y_up, h_dn)))
    compute(at(y_up, h_dn))
    from_dn(2, whole(at(y_dn, h_up)))
    compute(at(y_dn, h_up))
    arrived(4, low_half(at(y, h_op)))
    y_send(3, low_half(at(y, h_op)))
    arrived(5, high_half(at(y, h_op)))
    y_send(4, high_half(at(y, h_op)))
    from_up(2, whole(at(y_up, h_up)))
    compute(at(y_up, h_up))
    from_op(1, whole(at(y_op, h_dn)))
    compute(at(y_op, h_dn))
    from_op(2, whole(at(y_op, h_up)))
    compute(at(y_op, h_up))
    compute(at(y, h_op))
    start(21, biomass, halo_b.at[0], to_next)
    start(22, biomass, halo_b.at[1], to_prev)
    start(23, resources, halo_r.at[0], to_next)
    start(24, resources, halo_r.at[1], to_prev)
    from_dn(3, low_half(at(y_dn, h_op)))
    from_dn(4, high_half(at(y_dn, h_op)))
    compute(at(y_dn, h_op))
    from_up(3, low_half(at(y_up, h_op)))
    from_up(4, high_half(at(y_up, h_op)))
    compute(at(y_up, h_op))
    from_op(3, low_half(at(y_op, h_op)))
    from_op(4, high_half(at(y_op, h_op)))
    compute(at(y_op, h_op))

    def to_product(s, _):
        value = (mass[s] * flux[s]).astype(jnp.bfloat16).astype(jnp.float32)
        product[pl.ds(pl.multiple_of(s * ROWS, ROWS), ROWS), :] = value
        return 0

    lax.fori_loop(0, strains, to_product, 0, unroll=4)

    rows = ROWS // PARTS
    base = 25
    span = RING * block
    y_others = ((y_op, to_y_op), (y_up, to_y_up), (y_dn, to_y_dn))
    h_others = ((h_op, to_h_op), (h_up, to_h_up), (h_dn, to_h_dn))

    def all_rows(p):
        return pl.ds(p * rows, rows)

    def all_pairs(p):
        return pl.ds(p * rows // 2, rows // 2)

    def run(yy):
        return pl.ds(pl.multiple_of(yy * span, span), span)

    def pair(k, hh):
        at_h = pl.ds(pl.multiple_of(hh * block, block), block)
        return jnp.concatenate([reduced[2 * k, at_h], reduced[2 * k + 1, at_h]], axis=0)

    for p in range(PARTS):
        for q in range(p * rows, (p + 1) * rows):
            made = product[pl.ds(q, strains, stride=ROWS), :].astype(jnp.bfloat16)
            secreted = jnp.dot(sec, made, preferred_element_type=jnp.float32)
            used = consumed[pl.ds(q, blocks * block, stride=ROWS), :]
            net[q] = secreted - used
            for i, (yy, _) in enumerate(y_others):
                send_y[i, q] = encode(net[q, run(yy)])
        for i, (_, target) in enumerate(y_others):
            part = all_rows(p)
            start(base + 6 * p + i, send_y.at[i, part], sum_y.at[i, part], target)

    arrived(21, halo_b.at[0])
    arrived(22, halo_b.at[1])

    def update(s, _):
        m = mass[s]
        grown = gain[s] - maintenance[s]
        low = halo_b[0, s].astype(jnp.float32)
        high = halo_b[1, s].astype(jnp.float32)
        growth_out[s] = grown
        spread = motility[s] * laplace(m, low, high)
        biomass_out[s] = m + TIME_STEP * (m * grown + spread)
        return 0

    lax.fori_loop(0, strains, update, 0, unroll=2)
    stores = [
        pltpu.make_async_copy(growth_out, growth_hbm, store_sem.at[0]),
        pltpu.make_async_copy(biomass_out, biomass_hbm, store_sem.at[1]),
        pltpu.make_async_copy(resources_out, resources_hbm, store_sem.at[2]),
    ]
    stores[0].start()
    stores[1].start()

    for p in range(PARTS):
        for i in range(3):
            arrived(base + 6 * p + i, sum_y.at[i, all_rows(p)])
        for q in range(p * rows, (p + 1) * rows):
            others = decode(sum_y[0, q]) + decode(sum_y[1, q]) + decode(sum_y[2, q])
            reduced[q] = net[q, run(y)] + others
        for i, (hh, target) in enumerate(h_others):
            for j in range(p * rows // 2, (p + 1) * rows // 2):
                send_z[i, j] = encode(pair(j, hh))
            part = all_pairs(p)
            start(base + 6 * p + 3 + i, send_z.at[i, part], sum_z.at[i, part], target)

    arrived(23, halo_r.at[0])
    arrived(24, halo_r.at[1])
    for r in range(block):
        value = resources[r]
        spread = diffusivity[r] * laplace(value, halo_r[0, r], halo_r[1, r])
        resources_out[r] = value + TIME_STEP * (spread + supply[r])
    for p in range(PARTS):
        for i in range(3):
            arrived(base + 6 * p + 3 + i, sum_z.at[i, all_pairs(p)])
        for j in range(p * rows // 2, (p + 1) * rows // 2):
            others = decode(sum_z[0, j]) + decode(sum_z[1, j]) + decode(sum_z[2, j])
            total = pair(j, h) + others
            final[pl.ds(2 * j, block, stride=ROWS), :] = total[:block]
            final[pl.ds(2 * j + 1, block, stride=ROWS), :] = total[block:]
    for r in range(block):
        released = final[pl.ds(r * ROWS, ROWS), :]
        resources_out[r] = resources_out[r] + TIME_STEP * released
    stores[2].start()
    for c in started:
        c.wait_send()
    for store in stores:
        store.wait()


def store_kernel(a, b, c, a_out, b_out, c_out, a_mid, b_mid, c_mid, sem):
    chains = ((a, a_mid, a_out), (b, b_mid, b_out), (c, c_mid, c_out))
    loads = []
    stores = []
    for i, (src, mid, dst) in enumerate(chains):
        loads.append(pltpu.make_async_copy(src, mid, sem.at[0, i]))
        stores.append(pltpu.make_async_copy(mid, dst, sem.at[1, i]))
    for load in loads:
        load.start()
    for load, store in zip(loads, stores):
        load.wait()
        store.start()
    for store in stores:
        store.wait()


def per_device(
    biomass,
    resources,
    capacity,
    affinity,
    secretion,
    energy_yield,
    maintenance,
    motility,
    diffusivity,
    supply,
    n_space,
):
    strains, slab, plane = biomass.shape
    block = resources.shape[0]
    blocks = RING * RING
    tiles = plane // LANES

    def split(field):
        parts = field.reshape(field.shape[0], slab, tiles, LANES)
        return parts.transpose(0, 2, 1, 3).reshape(field.shape[0], ROWS, LANES)

    def join(field):
        parts = field.reshape(field.shape[0], tiles, slab, LANES)
        return parts.transpose(0, 2, 1, 3).reshape(field.shape[0], slab, plane)

    f32, bf16 = jnp.float32, jnp.bfloat16
    hbm = pl.BlockSpec(memory_space=pltpu.HBM)
    copies = 25 + 6 * PARTS
    outs = pl.pallas_call(
        functools.partial(kernel, n_space),
        out_shape=(
            jax.ShapeDtypeStruct((strains, ROWS, LANES), f32),
            jax.ShapeDtypeStruct((strains, ROWS, LANES), f32),
            jax.ShapeDtypeStruct((block, ROWS, LANES), f32),
        ),
        in_specs=[hbm] * 10,
        out_specs=(hbm,) * 3,
        scratch_shapes=[
            pltpu.VMEM((strains, ROWS, LANES), jnp.bfloat16),
            pltpu.VMEM((block, ROWS, LANES), f32),
            pltpu.VMEM(capacity.shape, f32),
            pltpu.VMEM(affinity.shape, f32),
            pltpu.VMEM((strains, blocks * block), jnp.bfloat16),
            pltpu.SMEM(energy_yield.shape, f32),
            pltpu.SMEM(maintenance.shape, f32),
            pltpu.SMEM(motility.shape, f32),
            pltpu.SMEM(diffusivity.shape, f32),
            pltpu.SMEM(supply.shape, f32),
            pltpu.VMEM((blocks, block, ROWS, LANES), jnp.bfloat16),
            pltpu.VMEM((strains, ROWS, LANES), f32),
            pltpu.VMEM((strains, LANES, LANES), f32),
            pltpu.VMEM((strains, LANES, LANES), f32),
            pltpu.VMEM((strains, ROWS, LANES), f32),
            pltpu.VMEM((strains, ROWS, LANES), f32),
            pltpu.VMEM((blocks * block * ROWS, LANES), f32),
            pltpu.VMEM((strains * ROWS, LANES), f32),
            pltpu.VMEM((ROWS, blocks * block, LANES), f32),
            pltpu.VMEM((3, ROWS, RING * block, LANES), bf16),
            pltpu.VMEM((3, ROWS, RING * block, LANES), bf16),
            pltpu.VMEM((ROWS, RING * block, LANES), f32),
            pltpu.VMEM((3, ROWS // 2, 2 * block, LANES), bf16),
            pltpu.VMEM((3, ROWS // 2, 2 * block, LANES), bf16),
            pltpu.VMEM((block * ROWS, LANES), f32),
            pltpu.VMEM((2, strains, ROWS, LANES), jnp.bfloat16),
            pltpu.VMEM((2, block, ROWS, LANES), f32),
            pltpu.SemaphoreType.DMA((copies,)),
            pltpu.SemaphoreType.DMA((copies,)),
            pltpu.SemaphoreType.DMA((10,)),
            pltpu.SemaphoreType.DMA((3,)),
            pltpu.VMEM((strains, ROWS, LANES), f32),
            pltpu.VMEM((strains, ROWS, LANES), f32),
            pltpu.VMEM((block, ROWS, LANES), f32),
        ],
        compiler_params=pltpu.CompilerParams(
            collective_id=0, has_side_effects=True, vmem_limit_bytes=67043328
        ),
    )(
        split(biomass),
        split(resources),
        capacity,
        affinity,
        secretion.T,
        energy_yield,
        maintenance,
        motility,
        diffusivity,
        supply,
    )
    outs = pl.pallas_call(
        store_kernel,
        out_shape=tuple(jax.ShapeDtypeStruct(out.shape, f32) for out in outs),
        in_specs=[hbm] * 3,
        out_specs=(hbm,) * 3,
        scratch_shapes=[
            *(pltpu.VMEM(out.shape, f32) for out in outs),
            pltpu.SemaphoreType.DMA((2, 3)),
        ],
        compiler_params=pltpu.CompilerParams(vmem_limit_bytes=67043328),
    )(*outs)
    return tuple(join(out) for out in outs)


def solution(mesh):
    return jax.shard_map(
        functools.partial(per_device, n_space=mesh.shape["space"]),
        mesh=mesh,
        in_specs=(
            P("species", "space", None),
            P("species", "space", None),
            P("species", None),
            P("species", None),
            P(None, "species"),
            P(),
            P("species"),
            P("species"),
            P("species"),
            P("species"),
        ),
        out_specs=(
            P("species", "space", None),
            P("species", "space", None),
            P("species", "space", None),
        ),
        check_vma=False,
    )
```

```python
import functools

import jax
import jax.numpy as jnp
from jax import lax
from jax.experimental import pallas as pl
from jax.experimental.pallas import tpu as pltpu
from jax.sharding import PartitionSpec as P

MESH = pl.DeviceIdType.MESH
RING = 4
GROUP = 4
UNROLL = 16
PIECES = (8, 8)
TIME_STEP = 0.25
SMALL = 2.0**-6
STEPS = 19.5
BOTTOM = 125.0
ROWS = 16
LANES = 128


def laplace(field, low, high):
    row = lax.broadcasted_iota(jnp.int32, (ROWS, LANES), 0)
    lane = lax.broadcasted_iota(jnp.int32, (ROWS, LANES), 1)
    odd = lax.rem(row, 2) == 1
    z = lax.rem(lane, 64)
    both = field + jnp.where(odd, low, high)
    beside_x = jnp.where(odd, pltpu.roll(both, 1, 0), pltpu.roll(both, ROWS - 1, 0))
    up = jnp.where(z == 63, field, pltpu.roll(field, LANES - 1, 1))
    down = jnp.where(z == 0, field, pltpu.roll(field, 1, 1))
    half = pltpu.roll(field, 64, 1)
    before = jnp.where(row < 2, field, pltpu.roll(half, 2, 0))
    after = jnp.where(row >= ROWS - 2, field, pltpu.roll(half, ROWS - 2, 0))
    beside_y = half + jnp.where(lane < 64, before, after)
    return beside_x + (beside_y + (up + down)) - 6.0 * field


def encode(value):
    level = jnp.log2(jnp.abs(value) * (1.0 / SMALL) + 1.0)
    code = jnp.exp2(level * STEPS - BOTTOM)
    return jnp.where(value < 0.0, -code, code).astype(jnp.bfloat16)


def decode(code):
    code = code.astype(jnp.float32)
    level = (jnp.log2(jnp.abs(code)) + BOTTOM) * (1.0 / STEPS)
    value = jnp.exp2(level) * SMALL - SMALL
    return jnp.where(code < 0.0, -value, value)


def kernel(
    n_space,
    biomass_in,
    resources_in,
    capacity_in,
    affinity_in,
    secretion_in,
    energy_yield_in,
    maintenance_in,
    motility_in,
    diffusivity_in,
    supply_in,
    growth_hbm,
    biomass_hbm,
    resources_hbm,
    biomass,
    resources,
    capacity,
    affinity,
    secretion,
    energy_yield,
    maintenance,
    motility,
    diffusivity,
    supply,
    seen,
    mass,
    shifts,
    slopes,
    flux,
    gain,
    consumed,
    product,
    net,
    send_y,
    sum_y,
    reduced,
    send_z,
    sum_z,
    final,
    halo_b,
    halo_r,
    send_sem,
    recv_sem,
    load_sem,
    store_sem,
    growth_out,
    biomass_out,
    resources_out,
):
    strains = biomass.shape[0]
    block = resources.shape[0]
    blocks = RING * RING
    half = block // 2
    me = lax.axis_index("species")
    place = lax.axis_index("space")
    y, h = lax.div(me, RING), lax.rem(me, RING)
    y_up, y_dn, y_op = (lax.rem(y + k, RING) for k in (1, 3, 2))
    h_up, h_dn, h_op = (lax.rem(h + k, RING) for k in (1, 3, 2))
    to_y_up = {"species": y_up * RING + h}
    to_y_dn = {"species": y_dn * RING + h}
    to_y_op = {"species": y_op * RING + h}
    to_h_up = {"species": y * RING + h_up}
    to_h_dn = {"species": y * RING + h_dn}
    to_h_op = {"species": y * RING + h_op}
    to_next = {"space": lax.rem(place + 1, n_space)}
    to_prev = {"space": lax.rem(place + n_space - 1, n_space)}

    barrier = pltpu.get_barrier_semaphore()
    for target in (to_h_up, to_h_dn, to_y_up, to_y_dn, to_y_op, to_next, to_prev):
        pl.semaphore_signal(barrier, inc=1, device_id=target, device_id_type=MESH)

    pairs = (
        (resources_in, resources),
        (biomass_in, biomass),
        (capacity_in, capacity),
        (affinity_in, affinity),
        (secretion_in, secretion),
        (energy_yield_in, energy_yield),
        (maintenance_in, maintenance),
        (motility_in, motility),
        (diffusivity_in, diffusivity),
        (supply_in, supply),
    )
    loads = [
        pltpu.make_async_copy(src, dst, load_sem.at[i])
        for i, (src, dst) in enumerate(pairs)
    ]
    for load in loads:
        load.start()
    loads[0].wait()
    seen[me] = resources[...].astype(jnp.bfloat16)

    pl.semaphore_wait(barrier, 7)

    started = []

    def copy(index, src, dst, target):
        return pltpu.make_async_remote_copy(
            src_ref=src,
            dst_ref=dst,
            send_sem=send_sem.at[index],
            recv_sem=recv_sem.at[index],
            device_id=target,
            device_id_type=MESH,
        )

    def start(index, src, dst, target):
        c = copy(index, src, dst, target)
        c.start()
        started.append(c)

    def arrived(index, ref):
        copy(index, ref, ref, to_y_up).wait_recv()

    def whole(b):
        return seen.at[b]

    def low_half(b):
        return seen.at[b, pl.ds(0, half)]

    def high_half(b):
        return seen.at[b, pl.ds(half, half)]

    def at(yy, hh):
        return yy * RING + hh

    def y_send(column, part):
        start(6 + 3 * column, part, part, to_y_up)
        start(7 + 3 * column, part, part, to_y_dn)
        start(8 + 3 * column, part, part, to_y_op)

    def from_dn(column, part):
        arrived(6 + 3 * column, part)

    def from_up(column, part):
        arrived(7 + 3 * column, part)

    def from_op(column, part):
        arrived(8 + 3 * column, part)

    def compute(b):
        def quarter(part, _):
            first_r = part * GROUP
            inverse = [
                1.0 / seen[b, first_r + r].astype(jnp.float32) for r in range(GROUP)
            ]
            es = [energy_yield[b * block + first_r + r] for r in range(GROUP)]

            def strain(i, sums):
                sums = list(sums)
                for k in range(UNROLL):
                    s = i * UNROLL + k
                    m = mass[s]
                    f = flux[s]
                    g = gain[s]
                    for r in range(GROUP):
                        row = pl.ds(b * block + first_r + r, 1)
                        slope = jnp.broadcast_to(slopes[s, row, :], (ROWS, LANES))
                        shift = jnp.broadcast_to(shifts[s, row, :], (ROWS, LANES))
                        u = 1.0 / (slope * inverse[r] + shift)
                        sums[r] = sums[r] + m * u
                        f = f + u
                        g = g + es[r] * u
                    flux[s] = f
                    gain[s] = g
                return tuple(sums)

            zero = jnp.zeros((ROWS, LANES), jnp.float32)
            sums = lax.fori_loop(0, strains // UNROLL, strain, (zero,) * GROUP)
            for r in range(GROUP):
                row = pl.multiple_of((b * block + first_r + r) * ROWS, ROWS)
                consumed[pl.ds(row, ROWS), :] = sums[r]
            return 0

        lax.fori_loop(0, block // GROUP, quarter, 0)

    start(0, low_half(me), low_half(me), to_h_up)
    start(3, high_half(me), high_half(me), to_h_dn)
    start(1, high_half(me), high_half(me), to_h_up)
    start(2, low_half(me), low_half(me), to_h_dn)
    y_send(0, whole(me))

    for load in loads[1:]:
        load.wait()
    mass[...] = biomass[...].astype(jnp.float32)
    pad = jnp.zeros((LANES - strains, LANES), jnp.float32)
    shift_t = jnp.concatenate([1.0 / capacity[...], pad], axis=0).T
    slope_t = jnp.concatenate([affinity[...] / capacity[...], pad], axis=0).T
    for s in range(strains):
        shifts[s] = jnp.broadcast_to(shift_t[:, s : s + 1], (LANES, LANES))
        slopes[s] = jnp.broadcast_to(slope_t[:, s : s + 1], (LANES, LANES))
    sec = jnp.concatenate([secretion[...].astype(jnp.float32), pad], axis=0).T
    sec = sec[:, :strains].astype(jnp.bfloat16)
    flux[...] = jnp.zeros_like(flux)
    gain[...] = jnp.zeros_like(gain)

    compute(me)
    from_dn(0, whole(at(y_dn, h)))
    compute(at(y_dn, h))
    from_up(0, whole(at(y_up, h)))
    compute(at(y_up, h))
    arrived(0, low_half(at(y, h_dn)))
    start(4, low_half(at(y, h_dn)), low_half(at(y, h_dn)), to_h_up)
    arrived(3, high_half(at(y, h_up)))
    start(5, high_half(at(y, h_up)), high_half(at(y, h_up)), to_h_dn)
    arrived(1, high_half(at(y, h_dn)))
    y_send(1, whole(at(y, h_dn)))
    arrived(2, low_half(at(y, h_up)))
    y_send(2, whole(at(y, h_up)))
    from_op(0, whole(at(y_op, h)))
    compute(at(y_op, h))
    compute(at(y, h_dn))
    compute(at(y, h_up))
    from_dn(1, whole(at(y_dn, h_dn)))
    compute(at(y_dn, h_dn))
    from_up(1, whole(at(y_up, h_dn)))
    compute(at(y_up, h_dn))
    from_dn(2, whole(at(y_dn, h_up)))
    compute(at(y_dn, h_up))
    arrived(4, low_half(at(y, h_op)))
    y_send(3, low_half(at(y, h_op)))
    arrived(5, high_half(at(y, h_op)))
    y_send(4, high_half(at(y, h_op)))
    from_up(2, whole(at(y_up, h_up)))
    compute(at(y_up, h_up))
    from_op(1, whole(at(y_op, h_dn)))
    compute(at(y_op, h_dn))
    from_op(2, whole(at(y_op, h_up)))
    compute(at(y_op, h_up))
    compute(at(y, h_op))
    start(21, biomass, halo_b.at[0], to_next)
    start(22, biomass, halo_b.at[1], to_prev)
    start(23, resources, halo_r.at[0], to_next)
    start(24, resources, halo_r.at[1], to_prev)
    from_dn(3, low_half(at(y_dn, h_op)))
    from_dn(4, high_half(at(y_dn, h_op)))
    compute(at(y_dn, h_op))
    from_up(3, low_half(at(y_up, h_op)))
    from_up(4, high_half(at(y_up, h_op)))
    compute(at(y_up, h_op))
    from_op(3, low_half(at(y_op, h_op)))
    from_op(4, high_half(at(y_op, h_op)))
    compute(at(y_op, h_op))

    def to_product(s, _):
        value = (mass[s] * flux[s]).astype(jnp.bfloat16).astype(jnp.float32)
        product[pl.ds(pl.multiple_of(s * ROWS, ROWS), ROWS), :] = value
        return 0

    lax.fori_loop(0, strains, to_product, 0, unroll=4)

    base = 25
    edges = [sum(PIECES[:p]) for p in range(len(PIECES) + 1)]
    span = RING * block
    y_others = ((y_op, to_y_op), (y_up, to_y_up), (y_dn, to_y_dn))
    h_others = ((h_op, to_h_op), (h_up, to_h_up), (h_dn, to_h_dn))

    def all_rows(p):
        return pl.ds(edges[p], PIECES[p])

    def all_pairs(p):
        return pl.ds(edges[p] // 2, PIECES[p] // 2)

    def run(yy):
        return pl.ds(pl.multiple_of(yy * span, span), span)

    def pair(k, hh):
        at_h = pl.ds(pl.multiple_of(hh * block, block), block)
        return jnp.concatenate([reduced[2 * k, at_h], reduced[2 * k + 1, at_h]], axis=0)

    for p in range(len(PIECES)):
        for q in range(edges[p], edges[p + 1]):
            made = product[pl.ds(q, strains, stride=ROWS), :].astype(jnp.bfloat16)
            secreted = jnp.dot(sec, made, preferred_element_type=jnp.float32)
            used = consumed[pl.ds(q, blocks * block, stride=ROWS), :]
            net[q] = secreted - used
            for i, (yy, _) in enumerate(y_others):
                send_y[i, q] = encode(net[q, run(yy)])
        for i, (_, target) in enumerate(y_others):
            part = all_rows(p)
            start(base + 6 * p + i, send_y.at[i, part], sum_y.at[i, part], target)

    arrived(21, halo_b.at[0])
    arrived(22, halo_b.at[1])

    def update(s, _):
        m = mass[s]
        grown = gain[s] - maintenance[s]
        low = halo_b[0, s].astype(jnp.float32)
        high = halo_b[1, s].astype(jnp.float32)
        growth_out[s] = grown
        spread = motility[s] * laplace(m, low, high)
        biomass_out[s] = m + TIME_STEP * (m * grown + spread)
        return 0

    lax.fori_loop(0, strains, update, 0, unroll=2)
    stores = [
        pltpu.make_async_copy(growth_out, growth_hbm, store_sem.at[0]),
        pltpu.make_async_copy(biomass_out, biomass_hbm, store_sem.at[1]),
        pltpu.make_async_copy(resources_out, resources_hbm, store_sem.at[2]),
    ]
    stores[0].start()
    stores[1].start()

    for p in range(len(PIECES)):
        for i in range(3):
            arrived(base + 6 * p + i, sum_y.at[i, all_rows(p)])
        for q in range(edges[p], edges[p + 1]):
            others = decode(sum_y[0, q]) + decode(sum_y[1, q]) + decode(sum_y[2, q])
            reduced[q] = net[q, run(y)] + others
        for i, (hh, target) in enumerate(h_others):
            for j in range(edges[p] // 2, edges[p + 1] // 2):
                send_z[i, j] = encode(pair(j, hh))
            part = all_pairs(p)
            start(base + 6 * p + 3 + i, send_z.at[i, part], sum_z.at[i, part], target)

    arrived(23, halo_r.at[0])
    arrived(24, halo_r.at[1])
    for r in range(block):
        value = resources[r]
        spread = diffusivity[r] * laplace(value, halo_r[0, r], halo_r[1, r])
        resources_out[r] = value + TIME_STEP * (spread + supply[r])
    for p in range(len(PIECES)):
        for i in range(3):
            arrived(base + 6 * p + 3 + i, sum_z.at[i, all_pairs(p)])
        for j in range(edges[p] // 2, edges[p + 1] // 2):
            others = decode(sum_z[0, j]) + decode(sum_z[1, j]) + decode(sum_z[2, j])
            total = pair(j, h) + others
            final[pl.ds(2 * j, block, stride=ROWS), :] = total[:block]
            final[pl.ds(2 * j + 1, block, stride=ROWS), :] = total[block:]
    for r in range(block):
        released = final[pl.ds(r * ROWS, ROWS), :]
        resources_out[r] = resources_out[r] + TIME_STEP * released
    stores[2].start()
    for c in started:
        c.wait_send()
    for store in stores:
        store.wait()


def store_kernel(a, b, c, a_out, b_out, c_out, a_mid, b_mid, c_mid, sem):
    chains = ((a, a_mid, a_out), (b, b_mid, b_out), (c, c_mid, c_out))
    loads = []
    stores = []
    for i, (src, mid, dst) in enumerate(chains):
        loads.append(pltpu.make_async_copy(src, mid, sem.at[0, i]))
        stores.append(pltpu.make_async_copy(mid, dst, sem.at[1, i]))
    for load in loads:
        load.start()
    for load, store in zip(loads, stores):
        load.wait()
        store.start()
    for store in stores:
        store.wait()


def per_device(
    biomass,
    resources,
    capacity,
    affinity,
    secretion,
    energy_yield,
    maintenance,
    motility,
    diffusivity,
    supply,
    n_space,
):
    strains, slab, plane = biomass.shape
    block = resources.shape[0]
    blocks = RING * RING
    tiles = plane // LANES

    def split(field):
        parts = field.reshape(field.shape[0], slab, tiles, LANES)
        return parts.transpose(0, 2, 1, 3).reshape(field.shape[0], ROWS, LANES)

    def join(field):
        parts = field.reshape(field.shape[0], tiles, slab, LANES)
        return parts.transpose(0, 2, 1, 3).reshape(field.shape[0], slab, plane)

    f32, bf16 = jnp.float32, jnp.bfloat16
    hbm = pl.BlockSpec(memory_space=pltpu.HBM)
    copies = 25 + 6 * len(PIECES)
    outs = pl.pallas_call(
        functools.partial(kernel, n_space),
        out_shape=(
            jax.ShapeDtypeStruct((strains, ROWS, LANES), f32),
            jax.ShapeDtypeStruct((strains, ROWS, LANES), f32),
            jax.ShapeDtypeStruct((block, ROWS, LANES), f32),
        ),
        in_specs=[hbm] * 10,
        out_specs=(hbm,) * 3,
        scratch_shapes=[
            pltpu.VMEM((strains, ROWS, LANES), jnp.bfloat16),
            pltpu.VMEM((block, ROWS, LANES), f32),
            pltpu.VMEM(capacity.shape, f32),
            pltpu.VMEM(affinity.shape, f32),
            pltpu.VMEM((strains, blocks * block), jnp.bfloat16),
            pltpu.SMEM(energy_yield.shape, f32),
            pltpu.SMEM(maintenance.shape, f32),
            pltpu.SMEM(motility.shape, f32),
            pltpu.SMEM(diffusivity.shape, f32),
            pltpu.SMEM(supply.shape, f32),
            pltpu.VMEM((blocks, block, ROWS, LANES), jnp.bfloat16),
            pltpu.VMEM((strains, ROWS, LANES), f32),
            pltpu.VMEM((strains, LANES, LANES), f32),
            pltpu.VMEM((strains, LANES, LANES), f32),
            pltpu.VMEM((strains, ROWS, LANES), f32),
            pltpu.VMEM((strains, ROWS, LANES), f32),
            pltpu.VMEM((blocks * block * ROWS, LANES), f32),
            pltpu.VMEM((strains * ROWS, LANES), f32),
            pltpu.VMEM((ROWS, blocks * block, LANES), f32),
            pltpu.VMEM((3, ROWS, RING * block, LANES), bf16),
            pltpu.VMEM((3, ROWS, RING * block, LANES), bf16),
            pltpu.VMEM((ROWS, RING * block, LANES), f32),
            pltpu.VMEM((3, ROWS // 2, 2 * block, LANES), bf16),
            pltpu.VMEM((3, ROWS // 2, 2 * block, LANES), bf16),
            pltpu.VMEM((block * ROWS, LANES), f32),
            pltpu.VMEM((2, strains, ROWS, LANES), jnp.bfloat16),
            pltpu.VMEM((2, block, ROWS, LANES), f32),
            pltpu.SemaphoreType.DMA((copies,)),
            pltpu.SemaphoreType.DMA((copies,)),
            pltpu.SemaphoreType.DMA((10,)),
            pltpu.SemaphoreType.DMA((3,)),
            pltpu.VMEM((strains, ROWS, LANES), f32),
            pltpu.VMEM((strains, ROWS, LANES), f32),
            pltpu.VMEM((block, ROWS, LANES), f32),
        ],
        compiler_params=pltpu.CompilerParams(
            collective_id=0, has_side_effects=True, vmem_limit_bytes=67043328
        ),
    )(
        split(biomass),
        split(resources),
        capacity,
        affinity,
        secretion.T,
        energy_yield,
        maintenance,
        motility,
        diffusivity,
        supply,
    )
    outs = pl.pallas_call(
        store_kernel,
        out_shape=tuple(jax.ShapeDtypeStruct(out.shape, f32) for out in outs),
        in_specs=[hbm] * 3,
        out_specs=(hbm,) * 3,
        scratch_shapes=[
            *(pltpu.VMEM(out.shape, f32) for out in outs),
            pltpu.SemaphoreType.DMA((2, 3)),
        ],
        compiler_params=pltpu.CompilerParams(vmem_limit_bytes=67043328),
    )(*outs)
    return tuple(join(out) for out in outs)


def solution(mesh):
    return jax.shard_map(
        functools.partial(per_device, n_space=mesh.shape["space"]),
        mesh=mesh,
        in_specs=(
            P("species", "space", None),
            P("species", "space", None),
            P("species", None),
            P("species", None),
            P(None, "species"),
            P(),
            P("species"),
            P("species"),
            P("species"),
            P("species"),
        ),
        out_specs=(
            P("species", "space", None),
            P("species", "space", None),
            P("species", "space", None),
        ),
        check_vma=False,
    )
```
